32 devices in a mesh: gx: 4 (over x, core), gy: 8 (over z, y).
Axes of the slice: x: 2, y: 2, z: 4, core: 2. Of those that a mesh axis runs over, the one named last changes fastest.
Arguments:
- fine_nodes: bfloat16 [4, 8, 512, 128], P('gx', 'gy'), may hold values from -6 to 6
- fine_edges: int32 [4, 8, 2, 1536], P('gx', 'gy'), may hold values from 0 to 1023, as said below
- fine_live: int32 [4, 8], P('gx', 'gy'), may hold values from 512 to 1536, as said below
- fine_halo: int32 [4, 8, 4, 1], P('gx', 'gy'), may hold values from 0 to 3, as said below
- pool_map: int32 [4, 8, 512], P('gx', 'gy'), may hold values from 0 to 255, as said below
- coarse_edges: int32 [4, 8, 2, 2048], P('gx', 'gy'), may hold values from 0 to 767, as said below
- coarse_halo: int32 [4, 8, 4, 1], P('gx', 'gy'), may hold values from 0 to 1, as said below
- fine_weights: bfloat16 [5, 128, 128], replicated, may hold values from -0.5 to 0.5
- fine_bias: float32 [128], replicated, may hold values from -3 to 3
- fine_gain: float32 [128], replicated, may hold values from 0.25 to 1.75
- coarse_weights: bfloat16 [2, 5, 128, 128], replicated, may hold values from -0.5 to 0.5
- coarse_bias: float32 [2, 128], replicated, may hold values from -3 to 3
- coarse_gain: float32 [2, 128], replicated, may hold values from 0.25 to 1.75
- cotangent: bfloat16 [4, 8, 512, 128], P('gx', 'gy'), may hold values from -6 to 6
Outputs:
- fine_out: bfloat16 [4, 8, 512, 128], P('gx', 'gy')
- grad_fine_weights: float32 [5, 128, 128], replicated
- grad_fine_bias: float32 [128], replicated
- grad_fine_gain: float32 [128], replicated
- grad_coarse_weights: float32 [2, 5, 128, 128], replicated
- grad_coarse_bias: float32 [2, 128], replicated
- grad_coarse_gain: float32 [2, 128], replicated
- grad_pooled: float32 [4, 8, 256, 128], P('gx', 'gy')
The draws below stay inside these ranges and needn't reach their ends.
Inputs may be any that keep to these rules, and one draw needn't show every extreme that they name: `fine_edges`: row 0 of each device's slots names senders: below 512 a node of the device, from 512 on a row of the four halo groups; row 1 names receivers among the device's 512 nodes. `fine_live`: A multiple of 512; in every draw some device has all 1536 slots live. `fine_halo`: block numbers of the device's fine nodes; within one device and direction they differ. `pool_map`: every coarse node of a device is named by at least one of its fine nodes. `coarse_edges`: row 0 names senders: below 256 a coarse node of the device, from 256 on a row of the four coarse halo groups; row 1 names receivers among the device's 256 coarse nodes. `coarse_halo`: block numbers of the device's coarse nodes.
All inputs are finite; a program needn't handle non-finite values.
Results may differ from the reference program's by a relative error of at most 0.009.
Values may be sent and summed in bfloat16 or wider, within the bound.
A program may use at most 64 MiB of HBM per device.

```python
import math
from functools import partial
import jax
import jax.numpy as jnp
from jax import lax

H = 128
BLOCK = 128
NF_DEV = 512
EDGE_BLOCK = 512
COARSE_STEPS = 2
EDGE_SLOTS = 1536
TURNS = 3
NC_DEV = 256
EC_DEV = 2048
FINE_HALO = 1
GRID_X = 4
GRID_Y = 8
FINE_NODES = 16384


def edge_draw(key, node_count, halo_count, slot_count):
    subkeys = jax.random.split(key, 4)
    grid_shape = (GRID_X, GRID_Y, slot_count)
    receivers = jax.random.randint(subkeys[0], grid_shape, 0, node_count)
    own_senders = jax.random.randint(subkeys[1], grid_shape, 0, node_count)
    remote = node_count + jax.random.randint(subkeys[2], grid_shape, 0, halo_count)
    senders = jnp.where(jax.random.randint(subkeys[3], grid_shape, 0, 4) == 0, remote, own_senders)
    return jnp.stack([senders, receivers], axis=2).astype(jnp.int32)


def distinct_blocks(key, block_count, chosen_count):
    scores = jax.random.randint(key, (GRID_X, GRID_Y, 4, block_count), 0, 1 << 20) * block_count + lax.iota(jnp.int32, block_count)
    ordered = jnp.argsort(scores, axis=-1, stable=True)
    return ordered[..., :chosen_count].astype(jnp.int32)


def draw_fine_edges(key, part):
    return edge_draw(jax.random.fold_in(key, 11), NF_DEV, 4 * FINE_HALO * BLOCK, EDGE_SLOTS)


def draw_coarse_edges(key, part):
    return edge_draw(jax.random.fold_in(key, 13), NC_DEV, 4 * BLOCK, EC_DEV)


def draw_fine_halo(key, part):
    return distinct_blocks(jax.random.fold_in(key, 15), NF_DEV // BLOCK, FINE_HALO)


def draw_coarse_halo(key, part):
    return distinct_blocks(jax.random.fold_in(key, 17), NC_DEV // BLOCK, 1)


def draw_pool_map(key, part):
    stride = NF_DEV // NC_DEV
    spots = lax.broadcasted_iota(jnp.int32, (GRID_X, GRID_Y, NF_DEV), 2)
    random_map = jax.random.randint(jax.random.fold_in(key, 19), (GRID_X, GRID_Y, NF_DEV), 0, NC_DEV)
    return jnp.where(spots % stride == 0, spots // stride, random_map).astype(jnp.int32)


def draw_fine_live(key, part):
    subkeys = jax.random.split(jax.random.fold_in(key, 21), 3)
    lowest = max(1, TURNS // 4)
    highest = max(lowest + 1, TURNS // 2 + 1)
    drawn = jax.random.randint(subkeys[0], (GRID_X, GRID_Y), lowest, highest)
    filled = jax.random.randint(subkeys[1], (GRID_X, GRID_Y), 0, 8) == 0
    chosen = jax.random.randint(subkeys[2], (), 0, GRID_X * GRID_Y)
    position = lax.broadcasted_iota(jnp.int32, (GRID_X, GRID_Y), 0) * GRID_Y + lax.broadcasted_iota(jnp.int32, (GRID_X, GRID_Y), 1)
    blocks = jnp.where(filled | (position == chosen), TURNS, drawn)
    return (blocks * EDGE_BLOCK).astype(jnp.int32)


def level_of(stream_key, dims, shards, least, largest):
    def one(dim, parts):
        heights = jax.random.uniform(jax.random.fold_in(jax.random.fold_in(stream_key, 6), dim), (parts,), jnp.float32, least / len(shards), largest / len(shards))
        return jnp.repeat(jnp.exp(heights), dims[dim] // parts).reshape((-1,) + (1,) * (len(dims) - dim - 1))

    factor_of = one(*shards[0])
    for cut in shards[1:]:
        factor_of = factor_of * one(*cut)
    return factor_of


def noise(stream_key, shape, scale, limit, cuts=(), held_as=jnp.bfloat16):
    level = level_of(stream_key, shape, cuts, -0.22, 0.18) if cuts else 1.0
    array = jax.random.normal(stream_key, shape, jnp.float32) * scale * level
    return jnp.minimum(jnp.maximum(array, -limit), limit).astype(held_as)


def setup_inputs(seed: int = 0) -> dict:
    key_list = jax.random.split(jax.random.key(seed), 15)
    return {
        "fine_nodes": noise(key_list[0], (GRID_X, GRID_Y, NF_DEV, H), 1.0, 6.0, ((0, 4), (1, 8))),
        "fine_edges": draw_fine_edges(jax.random.fold_in(key_list[14], 71), 0),
        "fine_live": draw_fine_live(jax.random.fold_in(key_list[14], 71), 0),
        "fine_halo": draw_fine_halo(jax.random.fold_in(key_list[14], 71), 0),
        "pool_map": draw_pool_map(jax.random.fold_in(key_list[14], 71), 0),
        "coarse_edges": draw_coarse_edges(jax.random.fold_in(key_list[14], 71), 0),
        "coarse_halo": draw_coarse_halo(jax.random.fold_in(key_list[14], 71), 0),
        "fine_weights": noise(key_list[7], (5, H, H), H ** -0.5, 0.5),
        "fine_bias": noise(key_list[8], (H,), 0.5, 3.0, (), jnp.float32),
        "fine_gain": jnp.clip(1.0 + 0.15 * jax.random.normal(key_list[9], (H,), jnp.float32), 0.25, 1.75),
        "coarse_weights": noise(key_list[10], (COARSE_STEPS, 5, H, H), H ** -0.5, 0.5),
        "coarse_bias": noise(key_list[11], (COARSE_STEPS, H), 0.5, 3.0, (), jnp.float32),
        "coarse_gain": jnp.clip(1.0 + 0.15 * jax.random.normal(key_list[12], (COARSE_STEPS, H), jnp.float32), 0.25, 1.75),
        "cotangent": noise(key_list[13], (GRID_X, GRID_Y, NF_DEV, H), 1.0, 6.0, ((0, 4), (1, 8))),
    }


EPSILON = 1e-05

def layer_norm(values):
    centred = values - lax.optimization_barrier(jnp.mean(values, axis=-1, keepdims=True))
    spread = lax.optimization_barrier(jnp.mean(centred * centred, axis=-1, keepdims=True))
    return centred * lax.rsqrt(spread + EPSILON)

def split_parts(values):
    high = values.astype(jnp.bfloat16)
    low = (values - high.astype(jnp.float32)).astype(jnp.bfloat16)
    return (high, low)

def contract_rows(left, right):
    high, low = split_parts(right)
    numbers = (((0,), (0,)), ((), ()))
    return lax.dot_general(left, high, numbers, preferred_element_type=jnp.float32) + lax.dot_general(left, low, numbers, preferred_element_type=jnp.float32)

def times_transpose(left, weight):
    high, low = split_parts(left)
    numbers = (((1,), (1,)), ((), ()))
    return lax.dot_general(high, weight, numbers, preferred_element_type=jnp.float32) + lax.dot_general(low, weight, numbers, preferred_element_type=jnp.float32)

def make_one_hot(pool_rows, coarse_count):
    return (pool_rows[:, None] == lax.iota(jnp.int32, coarse_count)[None, :]).astype(jnp.bfloat16)

def pick_blocks(node_rows, block_lists):
    features = node_rows.shape[-1]
    blocked = node_rows.reshape(-1, BLOCK, features)
    return blocked[block_lists].reshape(4, -1, features)

def put_blocks(returned, block_lists, row_count):
    features = returned.shape[-1]
    pieces = returned.reshape(-1, BLOCK, features)
    total = jnp.zeros((row_count // BLOCK, BLOCK, features), jnp.float32).at[block_lists.reshape(-1)].add(pieces)
    return total.reshape(row_count, features)

def slot_block(edge_list, live_slots, first_slot, block_width):
    senders = lax.dynamic_slice_in_dim(edge_list[0], first_slot, block_width)
    receivers = lax.dynamic_slice_in_dim(edge_list[1], first_slot, block_width)
    weights_live = (first_slot + lax.iota(jnp.int32, block_width) < live_slots).astype(jnp.float32)
    return (senders, receivers, weights_live)

def step_forward(node_rows, halo_rows, edge_list, live_slots, turn_count, weights, edge_bias, norm_gain, block_width):
    row_count = node_rows.shape[0]
    extended = jnp.concatenate([node_rows, halo_rows], axis=0)
    proj_send = jnp.dot(extended, weights[0], preferred_element_type=jnp.float32)
    proj_recv = jnp.dot(node_rows, weights[1], preferred_element_type=jnp.float32)

    def one_turn(turn_index, running):
        first_slot = (turn_index * block_width).astype(jnp.int32)
        senders, receivers, weights_live = slot_block(edge_list, live_slots, first_slot, block_width)
        hidden = jax.nn.silu(proj_send[senders] + proj_recv[receivers] + edge_bias).astype(jnp.bfloat16)
        message = jnp.dot(hidden, weights[2], preferred_element_type=jnp.float32) * weights_live[:, None]
        return running.at[receivers].add(message)
    summed = lax.fori_loop(0, turn_count, one_turn, jnp.zeros((row_count, proj_recv.shape[1]), jnp.float32))
    agg_low = summed.astype(jnp.bfloat16)
    node_pre = jnp.dot(node_rows, weights[3], preferred_element_type=jnp.float32) + jnp.dot(agg_low, weights[4], preferred_element_type=jnp.float32)
    output = (node_rows.astype(jnp.float32) + norm_gain * layer_norm(node_pre)).astype(jnp.bfloat16)
    return (output, (extended, proj_send, proj_recv, agg_low, node_pre))

def step_backward(upstream, node_rows, saved_state, edge_list, live_slots, turn_count, weights, edge_bias, norm_gain, block_width, want_input):
    extended, proj_send, proj_recv, agg_low, node_pre = saved_state
    row_count = node_rows.shape[0]
    features = proj_recv.shape[1]
    normed, norm_back = jax.vjp(layer_norm, node_pre)
    grad_gain = lax.optimization_barrier(jnp.sum(upstream * normed, axis=0))
    grad_pre = norm_back(upstream * norm_gain)[0]
    grad_self = contract_rows(node_rows, grad_pre)
    grad_agg_weight = contract_rows(agg_low, grad_pre)
    grad_agg = times_transpose(grad_pre, weights[4])

    def one_turn(turn_index, running):
        grad_send, grad_recv, grad_bias, grad_msg = running
        first_slot = (turn_index * block_width).astype(jnp.int32)
        senders, receivers, weights_live = slot_block(edge_list, live_slots, first_slot, block_width)
        pre_act = proj_send[senders] + proj_recv[receivers] + edge_bias
        hidden = jax.nn.silu(pre_act).astype(jnp.bfloat16)
        grad_message = grad_agg[receivers] * weights_live[:, None]
        grad_msg = grad_msg + contract_rows(hidden, grad_message)
        sigmoid = jax.nn.sigmoid(pre_act)
        grad_act = times_transpose(grad_message, weights[2]) * sigmoid * (1.0 + pre_act * (1.0 - sigmoid))
        return (grad_send.at[senders].add(grad_act), grad_recv.at[receivers].add(grad_act), grad_bias + lax.optimization_barrier(jnp.sum(grad_act, axis=0)), grad_msg)
    start_state = (jnp.zeros(proj_send.shape, jnp.float32), jnp.zeros(proj_recv.shape, jnp.float32), jnp.zeros((features,), jnp.float32), jnp.zeros((features, features), jnp.float32))
    grad_send, grad_recv, grad_bias, grad_msg = lax.fori_loop(0, turn_count, one_turn, start_state)
    grad_weights = jnp.stack([contract_rows(extended, grad_send), contract_rows(node_rows, grad_recv), grad_msg, grad_self, grad_agg_weight])
    if not want_input:
        return ((grad_weights, grad_bias, grad_gain), None, None)
    grad_ext = times_transpose(grad_send, weights[0])
    grad_nodes = upstream + times_transpose(grad_pre, weights[3]) + times_transpose(grad_recv, weights[1]) + grad_ext[:row_count]
    return ((grad_weights, grad_bias, grad_gain), grad_nodes, grad_ext[row_count:])

def from_lower(values, axis):
    length = values.shape[axis]
    zero_part = jnp.zeros_like(lax.slice_in_dim(values, 0, 1, axis=axis))
    return jnp.concatenate([zero_part, lax.slice_in_dim(values, 0, length - 1, axis=axis)], axis=axis)

def from_upper(values, axis):
    length = values.shape[axis]
    zero_part = jnp.zeros_like(lax.slice_in_dim(values, 0, 1, axis=axis))
    return jnp.concatenate([lax.slice_in_dim(values, 1, length, axis=axis), zero_part], axis=axis)

def assemble(grid_rows, block_lists):
    sends = jax.vmap(jax.vmap(pick_blocks))(grid_rows, block_lists)
    groups = [from_lower(sends[:, :, 1], 0), from_upper(sends[:, :, 0], 0), from_lower(sends[:, :, 3], 1), from_upper(sends[:, :, 2], 1)]
    return jnp.concatenate(groups, axis=2)

def assemble_back(halo_grads, block_lists, row_count):
    split = halo_grads.reshape(halo_grads.shape[:2] + (4, -1, halo_grads.shape[-1]))
    returned = jnp.stack([from_lower(split[:, :, 1], 0), from_upper(split[:, :, 0], 0), from_lower(split[:, :, 3], 1), from_upper(split[:, :, 2], 1)], axis=2)
    return jax.vmap(jax.vmap(partial(put_blocks, row_count=row_count)))(returned, block_lists)

def sum_devices(values):
    return lax.optimization_barrier(jnp.sum(values, axis=0))

def reference(fine_nodes, fine_edges, fine_live, fine_halo, pool_map, coarse_edges, coarse_halo, fine_weights, fine_bias, fine_gain, coarse_weights, coarse_bias, coarse_gain, cotangent):
    device_count = GRID_X * GRID_Y
    fine_turns = EDGE_SLOTS // EDGE_BLOCK
    coarse_slots = EC_DEV
    coarse_turns = EC_DEV // EDGE_BLOCK
    loss_scale = 1.0 / math.sqrt(FINE_NODES)

    def flatten(values):
        return values.reshape((device_count,) + values.shape[2:])

    def gridded(values):
        return values.reshape((GRID_X, GRID_Y) + values.shape[1:])
    fine_ext = flatten(assemble(fine_nodes, fine_halo))
    flat_nodes = flatten(fine_nodes)
    flat_edges = flatten(fine_edges)
    flat_live = flatten(fine_live)
    flat_pool = flatten(pool_map)
    flat_coarse_edges = flatten(coarse_edges)
    flat_cot = flatten(cotangent)

    def fine_ahead(device_item):
        node_rows, halo_rows, edge_list, live_slots = device_item
        return step_forward(node_rows, halo_rows, edge_list, live_slots, fine_turns, fine_weights, fine_bias, fine_gain, EDGE_BLOCK)[0]
    fine_mid = lax.map(fine_ahead, (flat_nodes, fine_ext, flat_edges, flat_live))

    def pooling(device_item):
        mid_rows, pool_rows = device_item
        one_hot = make_one_hot(pool_rows, NC_DEV)
        pooled_sums = lax.dot_general(one_hot, mid_rows, (((0,), (0,)), ((), ())), preferred_element_type=jnp.float32)
        counts = lax.optimization_barrier(jnp.sum(one_hot, axis=0, dtype=jnp.float32))
        return ((pooled_sums / counts[:, None]).astype(jnp.bfloat16), counts)
    current, counts = lax.map(pooling, (fine_mid, flat_pool))

    def coarse_ahead(step_index, device_item):
        node_rows, halo_rows, edge_list = device_item
        return step_forward(node_rows, halo_rows, edge_list, coarse_slots, coarse_turns, coarse_weights[step_index], coarse_bias[step_index], coarse_gain[step_index], EDGE_BLOCK)[0]
    states = []
    for step_index in range(COARSE_STEPS):
        ext_now = flatten(assemble(gridded(current), coarse_halo))
        states.append((current, ext_now))
        current = lax.map(partial(coarse_ahead, step_index), (current, ext_now, flat_coarse_edges))

    def unpooling(device_item):
        mid_rows, pool_rows, coarse_rows = device_item
        lifted = jnp.dot(make_one_hot(pool_rows, NC_DEV), coarse_rows, preferred_element_type=jnp.float32)
        return (mid_rows.astype(jnp.float32) + lifted).astype(jnp.bfloat16)
    fine_out = lax.map(unpooling, (fine_mid, flat_pool, current))

    def coarse_seed(device_item):
        cot_rows, pool_rows = device_item
        return jax.ops.segment_sum(cot_rows.astype(jnp.float32) * loss_scale, pool_rows, num_segments=NC_DEV)
    upstream = lax.map(coarse_seed, (flat_cot, flat_pool))

    def coarse_behind(step_index, device_item):
        grad_rows, node_rows, halo_rows, edge_list = device_item
        saved_state = step_forward(node_rows, halo_rows, edge_list, coarse_slots, coarse_turns, coarse_weights[step_index], coarse_bias[step_index], coarse_gain[step_index], EDGE_BLOCK)[1]
        return step_backward(grad_rows, node_rows, saved_state, edge_list, coarse_slots, coarse_turns, coarse_weights[step_index], coarse_bias[step_index], coarse_gain[step_index], EDGE_BLOCK, True)
    coarse_terms = [None] * COARSE_STEPS
    for step_index in reversed(range(COARSE_STEPS)):
        inputs_now, ext_now = states[step_index]
        step_terms, grad_nodes, grad_halo = lax.map(partial(coarse_behind, step_index), (upstream, inputs_now, ext_now, flat_coarse_edges))
        upstream = grad_nodes + flatten(assemble_back(gridded(grad_halo), coarse_halo, NC_DEV))
        coarse_terms[step_index] = jax.tree.map(sum_devices, step_terms)
    grad_pooled = gridded(upstream * math.sqrt(FINE_NODES))

    def fine_behind(device_item):
        node_rows, halo_rows, edge_list, live_slots, cot_rows, pool_rows, coarse_up, coarse_counts = device_item
        saved_state = step_forward(node_rows, halo_rows, edge_list, live_slots, fine_turns, fine_weights, fine_bias, fine_gain, EDGE_BLOCK)[1]
        direct = cot_rows.astype(jnp.float32) * loss_scale
        fine_seed = direct + (coarse_up / coarse_counts[:, None])[pool_rows]
        return step_backward(fine_seed, node_rows, saved_state, edge_list, live_slots, fine_turns, fine_weights, fine_bias, fine_gain, EDGE_BLOCK, False)[0]
    fine_terms = jax.tree.map(sum_devices, lax.map(fine_behind, (flat_nodes, fine_ext, flat_edges, flat_live, flat_cot, flat_pool, upstream, counts)))
    grad_coarse_weights = jnp.stack([entry[0] for entry in coarse_terms])
    grad_coarse_bias = jnp.stack([entry[1] for entry in coarse_terms])
    grad_coarse_gain = jnp.stack([entry[2] for entry in coarse_terms])
    return (gridded(fine_out), fine_terms[0], fine_terms[1], fine_terms[2], grad_coarse_weights, grad_coarse_bias, grad_coarse_gain, grad_pooled)
```

```python
import math

import jax
import jax.numpy as jnp
from jax import lax
from jax.sharding import PartitionSpec as P

BLOCK = 128
EDGE_BLOCK = 512
COARSE_STEPS = 2
NC_DEV = 256


EPSILON = 1e-05


def extended_2(x, sides, width):
    for axis, dim in sides:
        peers, length = (lax.axis_size(axis), x.shape[dim])
        up = [(i, (i + 1) % peers) for i in range(peers - 1)]
        down = [(j, i) for i, j in up]
        last = lax.slice_in_dim(x, length - width, length, axis=dim)
        initial = lax.slice_in_dim(x, 0, width, axis=dim)
        before = lax.ppermute(last, axis, up)
        after = lax.ppermute(initial, axis, down)
        x = jnp.concatenate([before, x, after], axis=dim)
    return x


def layer_norm(values):
    centred = values - jnp.mean(values, axis=-1, keepdims=True)
    spread = jnp.mean(centred * centred, axis=-1, keepdims=True)
    return centred * lax.rsqrt(spread + EPSILON)


def split_parts(values):
    high = values.astype(jnp.bfloat16)
    low = (values - high.astype(jnp.float32)).astype(jnp.bfloat16)
    return (high, low)


def contract_rows(left, right):
    high, low = split_parts(right)
    numbers = (((0,), (0,)), ((), ()))
    return lax.dot_general(
        left, high, numbers, preferred_element_type=jnp.float32
    ) + lax.dot_general(left, low, numbers, preferred_element_type=jnp.float32)


def times_transpose(left, weight):
    high, low = split_parts(left)
    numbers = (((1,), (1,)), ((), ()))
    return lax.dot_general(
        high, weight, numbers, preferred_element_type=jnp.float32
    ) + lax.dot_general(low, weight, numbers, preferred_element_type=jnp.float32)


def make_one_hot(pool_rows, coarse_count):
    return (pool_rows[:, None] == lax.iota(jnp.int32, coarse_count)[None, :]).astype(jnp.bfloat16)


def pick_blocks(node_rows, block_lists):
    features = node_rows.shape[-1]
    blocked = node_rows.reshape(-1, BLOCK, features)
    return blocked[block_lists].reshape(4, -1, features)


def put_blocks(returned, block_lists, row_count):
    features = returned.shape[-1]
    total = (
        jnp.zeros((row_count // BLOCK, BLOCK, features), jnp.float32)
        .at[block_lists.reshape(-1)]
        .add(returned)
    )
    return total.reshape(row_count, features)


def slot_block(edge_list, live_slots, first_slot, block_width):
    senders = lax.dynamic_slice_in_dim(edge_list[0], first_slot, block_width)
    receivers = lax.dynamic_slice_in_dim(edge_list[1], first_slot, block_width)
    weights_live = (first_slot + lax.iota(jnp.int32, block_width) < live_slots).astype(jnp.float32)
    return (senders, receivers, weights_live)


def dot(left, right):
    return jnp.dot(left, right, preferred_element_type=jnp.float32)


def dot_rows(left, right):
    return lax.dot_general(left, right, (((0,), (0,)), ((), ())), preferred_element_type=jnp.float32)


def pick_matrix(edge_list, live_slots, ext_count, own_count):
    live = lax.iota(jnp.int32, edge_list.shape[1]) < live_slots
    senders = jnp.where(live, edge_list[0], -1)
    receivers = jnp.where(live, edge_list[1], -1)
    return jnp.concatenate([make_one_hot(senders, ext_count), make_one_hot(receivers, own_count)], axis=1)


def step_forward(node_rows, halo_rows, picks, weights, edge_bias, norm_gain):
    extended = jnp.concatenate([node_rows, halo_rows], axis=0)
    ext_count = extended.shape[0]
    table = jnp.concatenate([dot(extended, weights[0]), dot(node_rows, weights[1]) + edge_bias], axis=0)
    pre_act = dot(picks, table.astype(jnp.bfloat16))
    gate = jax.nn.sigmoid(pre_act)
    hidden = (pre_act * gate).astype(jnp.bfloat16)
    slope = gate * (1.0 + pre_act * (1.0 - gate))
    high, low = split_parts(dot_rows(picks[:, ext_count:], hidden))
    agg_low = (dot(high, weights[2]) + dot(low, weights[2])).astype(jnp.bfloat16)
    node_pre = dot(node_rows, weights[3]) + dot(agg_low, weights[4])
    output = (node_rows.astype(jnp.float32) + norm_gain * layer_norm(node_pre)).astype(jnp.bfloat16)
    return (output, (extended, high, slope, agg_low, node_pre))


def step_backward(upstream, node_rows, saved_state, picks, weights, norm_gain, want_input):
    extended, high, slope, agg_low, node_pre = saved_state
    row_count, ext_count = node_rows.shape[0], extended.shape[0]
    normed, norm_back = jax.vjp(layer_norm, node_pre)
    grad_gain = jnp.sum(upstream * normed, axis=0)
    grad_pre = norm_back(upstream * norm_gain)[0]
    grad_agg = times_transpose(grad_pre, weights[4])
    grad_hidden = times_transpose(grad_agg, weights[2])
    grad_act = dot(picks[:, ext_count:], grad_hidden.astype(jnp.bfloat16)) * slope
    gathered = dot_rows(picks, grad_act.astype(jnp.bfloat16))
    grad_send, grad_recv = gathered[:ext_count], gathered[ext_count:]
    grad_bias = jnp.sum(grad_recv, axis=0)
    grad_weights = jnp.stack(
        [
            contract_rows(extended, grad_send),
            contract_rows(node_rows, grad_recv),
            contract_rows(high, grad_agg),
            contract_rows(node_rows, grad_pre),
            contract_rows(agg_low, grad_pre),
        ]
    )
    if not want_input:
        return ((grad_weights, grad_bias, grad_gain), None, None)
    grad_ext = times_transpose(grad_send, weights[0])
    grad_nodes = (
        upstream
        + times_transpose(grad_pre, weights[3])
        + times_transpose(grad_recv, weights[1])
        + grad_ext[:row_count]
    )
    return ((grad_weights, grad_bias, grad_gain), grad_nodes, grad_ext[row_count:])


def fine_exchange(node_rows, block_lists):
    sends = pick_blocks(node_rows, block_lists)
    across = extended_2(sends[0:2], (("gx", 0),), 1)
    along = extended_2(sends[2:4], (("gy", 0),), 1)
    return jnp.concatenate([across[0], across[3], along[0], along[3]], axis=0)


def coarse_exchange(node_rows, block_lists):
    sends = pick_blocks(node_rows, block_lists)
    across = extended_2(sends[0:2], (("gx", 0),), 1)
    along = extended_2(sends[2:4], (("gy", 0),), 1)
    return jnp.concatenate([across[0], across[3], along[0], along[3]], axis=0)


def coarse_return(halo_grads, block_lists, row_count):
    split = halo_grads.reshape(4, -1, halo_grads.shape[-1])
    across = extended_2(split[0:2].astype(jnp.bfloat16), (("gx", 0),), 1).astype(jnp.float32)
    along = extended_2(split[2:4].astype(jnp.bfloat16), (("gy", 0),), 1).astype(jnp.float32)
    returned = jnp.stack([across[0], across[3], along[0], along[3]])
    return put_blocks(returned, block_lists, row_count)


def body(
    fine_nodes,
    fine_edges,
    fine_live,
    fine_halo,
    pool_map,
    coarse_edges,
    coarse_halo,
    fine_weights,
    fine_bias,
    fine_gain,
    coarse_weights,
    coarse_bias,
    coarse_gain,
    cotangent,
):
    node_rows = fine_nodes[0, 0]
    edge_list = fine_edges[0, 0]
    live_slots = fine_live[0, 0]
    pool_rows = pool_map[0, 0]
    coarse_list = coarse_edges[0, 0]
    coarse_blocks = coarse_halo[0, 0]
    coarse_slots = coarse_list.shape[1]
    halo_rows = fine_exchange(node_rows, fine_halo[0, 0])
    fine_picks = pick_matrix(edge_list, live_slots, node_rows.shape[0] + halo_rows.shape[0], node_rows.shape[0])
    coarse_picks = pick_matrix(coarse_list, coarse_slots, NC_DEV + 4 * BLOCK, NC_DEV)
    fine_mid, fine_saved = step_forward(
        node_rows,
        halo_rows,
        fine_picks,
        fine_weights,
        fine_bias,
        fine_gain,
    )
    one_hot = make_one_hot(pool_rows, NC_DEV)
    pooled_sums = lax.dot_general(
        one_hot, fine_mid, (((0,), (0,)), ((), ())), preferred_element_type=jnp.float32
    )
    counts = jnp.sum(one_hot, axis=0, dtype=jnp.float32)
    current = (pooled_sums / counts[:, None]).astype(jnp.bfloat16)
    states = []
    for step_index in range(COARSE_STEPS):
        coarse_rows = coarse_exchange(current, coarse_blocks)
        following, saved_state = step_forward(
            current,
            coarse_rows,
            coarse_picks,
            coarse_weights[step_index],
            coarse_bias[step_index],
            coarse_gain[step_index],
        )
        states.append((current, saved_state))
        current = following
    lifted = jnp.dot(one_hot, current, preferred_element_type=jnp.float32)
    fine_out = (fine_mid.astype(jnp.float32) + lifted).astype(jnp.bfloat16)
    total_nodes = node_rows.shape[0] * lax.axis_size("gx") * lax.axis_size("gy")
    loss_scale = 1.0 / math.sqrt(total_nodes)
    direct = cotangent[0, 0].astype(jnp.float32) * loss_scale
    upstream = dot_rows(one_hot, cotangent[0, 0]) * loss_scale
    coarse_terms = [None] * COARSE_STEPS
    for step_index in reversed(range(COARSE_STEPS)):
        inputs_now, saved_state = states[step_index]
        step_terms, grad_nodes, grad_halo = step_backward(
            upstream,
            inputs_now,
            saved_state,
            coarse_picks,
            coarse_weights[step_index],
            coarse_gain[step_index],
            True,
        )
        upstream = grad_nodes + coarse_return(grad_halo, coarse_blocks, NC_DEV)
        coarse_terms[step_index] = step_terms
    grad_pooled = upstream * math.sqrt(total_nodes)
    coarse_stacked = (
        jnp.stack([entry[0] for entry in coarse_terms]),
        jnp.stack([entry[1] for entry in coarse_terms]),
        jnp.stack([entry[2] for entry in coarse_terms]),
    )
    fine_seed = direct + dot(one_hot, (upstream / counts[:, None]).astype(jnp.bfloat16))
    fine_terms = step_backward(
        fine_seed,
        node_rows,
        fine_saved,
        fine_picks,
        fine_weights,
        fine_gain,
        False,
    )[0]
    everything = lax.psum(
        (
            fine_terms[0],
            fine_terms[1],
            fine_terms[2],
            coarse_stacked[0],
            coarse_stacked[1],
            coarse_stacked[2],
        ),
        ("gx", "gy"),
    )
    fine_total = everything[0:3]
    coarse_total = everything[3:6]
    return (
        fine_out[None, None],
        fine_total[0],
        fine_total[1],
        fine_total[2],
        coarse_total[0],
        coarse_total[1],
        coarse_total[2],
        grad_pooled[None, None],
    )


def solution(mesh):
    return jax.shard_map(
        body,
        mesh=mesh,
        in_specs=(
            P("gx", "gy", None, None),
            P("gx", "gy", None, None),
            P("gx", "gy"),
            P("gx", "gy", None, None),
            P("gx", "gy", None),
            P("gx", "gy", None, None),
            P("gx", "gy", None, None),
            P(),
            P(),
            P(),
            P(),
            P(),
            P(),
            P("gx", "gy", None, None),
        ),
        out_specs=(
            P("gx", "gy", None, None),
            P(),
            P(),
            P(),
            P(),
            P(),
            P(),
            P("gx", "gy", None, None),
        ),
        check_vma=False,
    )
```
